128 devices in a mesh: ctx: 64 (over z, x, y), wsh: 2 (over core).
Axes of the slice: x: 4, y: 4, z: 4, core: 2. Of those that a mesh axis runs over, the one named last changes fastest.
Arguments:
- block_input: bfloat16 [2, 8192, 640], P('wsh', 'ctx'), may hold values from -6 to 6
- cotangent: float32 [2, 8192, 640], P('wsh', 'ctx'), may hold values from -6 to 6
- pair_blocks: int32 [64, 2], replicated, may hold values from 0 to 127, as said below
- w_query: bfloat16 [640, 1024], P(None, 'wsh'), may hold values from -0.25 to 0.25
- w_key: bfloat16 [640, 256], P(None, 'wsh'), may hold values from -0.25 to 0.25
- w_value: bfloat16 [640, 256], P(None, 'wsh'), may hold values from -0.25 to 0.25
- w_out: bfloat16 [1024, 640], P('wsh'), may hold values from -0.1875 to 0.1875
- w_gate: bfloat16 [640, 2048], P(None, 'wsh'), may hold values from -0.25 to 0.25
- w_up: bfloat16 [640, 2048], P(None, 'wsh'), may hold values from -0.25 to 0.25
- w_down: bfloat16 [2048, 640], P('wsh'), may hold values from -0.125 to 0.125
- attn_pre_gain: bfloat16 [640], P('wsh'), may hold values from -0.3984375 to 0.59765625
- query_gain: bfloat16 [256], P('wsh'), may hold values from -0.3984375 to 0.59765625
- key_gain: bfloat16 [256], P('wsh'), may hold values from -0.3984375 to 0.59765625
- attn_post_gain: bfloat16 [640], P('wsh'), may hold values from -0.3984375 to 0.59765625
- ffw_pre_gain: bfloat16 [640], P('wsh'), may hold values from -0.3984375 to 0.59765625
- ffw_post_gain: bfloat16 [640], P('wsh'), may hold values from -0.3984375 to 0.59765625
Outputs:
- block_output: float32 [2, 8192, 640], P('wsh', 'ctx')
- input_grad: float32 [2, 8192, 640], P('wsh', 'ctx')
- w_query_grad: float32 [640, 1024], P(None, 'wsh')
- w_key_grad: float32 [640, 256], P(None, 'wsh')
- w_value_grad: float32 [640, 256], P(None, 'wsh')
- w_out_grad: float32 [1024, 640], P('wsh')
- w_gate_grad: float32 [640, 2048], P(None, 'wsh')
- w_up_grad: float32 [640, 2048], P(None, 'wsh')
- w_down_grad: float32 [2048, 640], P('wsh')
- attn_pre_gain_grad: float32 [640], P('wsh')
- query_gain_grad: float32 [256], P('wsh')
- key_gain_grad: float32 [256], P('wsh')
- attn_post_gain_grad: float32 [640], P('wsh')
- ffw_pre_gain_grad: float32 [640], P('wsh')
- ffw_post_gain_grad: float32 [640], P('wsh')
The draws below stay inside these ranges and needn't reach their ends.
Inputs may be any that keep to these rules, and one draw needn't show every extreme that they name: `pair_blocks`: row r holds a block b and its mirror 2 * 64 - 1 - b, in the order in which index r of ctx stores them; over all rows every one of the 128 blocks appears exactly once.
All inputs are finite; a program needn't handle non-finite values.
Results may differ from the reference program's by a relative error of at most 0.018.
Values may be sent and summed in bfloat16 or wider, within the bound.
No kernel may reach another device: no remote copies, remote signals or barrier semaphores. Data moves between devices by JAX's collectives and lax.ppermute only.
A program may use at most 192 MiB of HBM per device.

```python
import jax
import jax.numpy as jnp
from jax import lax

D = 640
HEADS = 4
HDIM = 256
FF = 2048
TOK_DEV = 128
RANKS = 64
SEQ = 8192
SEQS = 2
N_WSH = 2


def draw_pair_blocks(key, part):
    first = jax.random.permutation(jax.random.fold_in(key, 11), RANKS).astype(jnp.int32)
    flipped = jax.random.randint(jax.random.fold_in(key, 12), (RANKS,), 0, 2).astype(jnp.int32)
    mirror = 2 * RANKS - 1 - first
    lower = jnp.where(flipped == 1, mirror, first)
    upper = jnp.where(flipped == 1, first, mirror)
    return jnp.stack([lower, upper], axis=1).astype(jnp.int32)


def block_scale(key, dims, split, smallest, largest):
    loudness = 1.0
    for dim, shards_of in split:
        steps = jax.random.uniform(jax.random.fold_in(jax.random.fold_in(key, 6), dim), (shards_of,), jnp.float32, smallest / len(split), largest / len(split))
        loudness = loudness * jnp.repeat(jnp.exp(steps), dims[dim] // shards_of).reshape((-1,) + (1,) * (len(dims) - 1 - dim))
    return loudness


def noise(own_key, shape, scale, reach, pieces=(), kind=jnp.bfloat16):
    factor_of = block_scale(own_key, shape, pieces, -0.22, 0.18) if pieces else 1.0
    entries = jax.random.normal(own_key, shape, jnp.float32) * scale * factor_of
    return jnp.minimum(jnp.maximum(entries, -reach), reach).astype(kind)


def setup_inputs(seed: int = 0) -> dict:
    key_of = jax.random.split(jax.random.key(seed), 17)
    return {
        "block_input": noise(key_of[0], (SEQS, SEQ, D), 1.0, 6.0, ((0, 2), (1, 64))),
        "cotangent": noise(key_of[1], (SEQS, SEQ, D), 1.0, 6.0, ((0, 2), (1, 64)), jnp.float32),
        "pair_blocks": draw_pair_blocks(jax.random.fold_in(key_of[16], 71), 0),
        "w_query": noise(key_of[3], (D, HEADS * HDIM), D ** -0.5, 0.25, ((1, 2),)),
        "w_key": noise(key_of[4], (D, HDIM), D ** -0.5, 0.25, ((1, 2),)),
        "w_value": noise(key_of[5], (D, HDIM), D ** -0.5, 0.25, ((1, 2),)),
        "w_out": noise(key_of[6], (HEADS * HDIM, D), (HEADS * HDIM) ** -0.5, 0.1875, ((0, 2),)),
        "w_gate": noise(key_of[7], (D, FF), D ** -0.5, 0.25, ((1, 2),)),
        "w_up": noise(key_of[8], (D, FF), D ** -0.5, 0.25, ((1, 2),)),
        "w_down": noise(key_of[9], (FF, D), FF ** -0.5, 0.125, ((0, 2),)),
        "attn_pre_gain": jnp.clip(-0.3984375 + 0.99609375 * jax.random.uniform(key_of[10], (D,), jnp.float32) ** block_scale(key_of[10], (D,), ((0, 2),), -0.2, 0.2), -0.3984375, 0.59765625).astype(jnp.bfloat16),
        "query_gain": jnp.clip(-0.3984375 + 0.99609375 * jax.random.uniform(key_of[11], (HDIM,), jnp.float32) ** block_scale(key_of[11], (HDIM,), ((0, 2),), -0.2, 0.2), -0.3984375, 0.59765625).astype(jnp.bfloat16),
        "key_gain": jnp.clip(-0.3984375 + 0.99609375 * jax.random.uniform(key_of[12], (HDIM,), jnp.float32) ** block_scale(key_of[12], (HDIM,), ((0, 2),), -0.2, 0.2), -0.3984375, 0.59765625).astype(jnp.bfloat16),
        "attn_post_gain": jnp.clip(-0.3984375 + 0.99609375 * jax.random.uniform(key_of[13], (D,), jnp.float32) ** block_scale(key_of[13], (D,), ((0, 2),), -0.2, 0.2), -0.3984375, 0.59765625).astype(jnp.bfloat16),
        "ffw_pre_gain": jnp.clip(-0.3984375 + 0.99609375 * jax.random.uniform(key_of[14], (D,), jnp.float32) ** block_scale(key_of[14], (D,), ((0, 2),), -0.2, 0.2), -0.3984375, 0.59765625).astype(jnp.bfloat16),
        "ffw_post_gain": jnp.clip(-0.3984375 + 0.99609375 * jax.random.uniform(key_of[15], (D,), jnp.float32) ** block_scale(key_of[15], (D,), ((0, 2),), -0.2, 0.2), -0.3984375, 0.59765625).astype(jnp.bfloat16),
    }


epsilon = 1e-06
theta_base = 1000000.0

def rounded(values):
    return lax.optimization_barrier(values.astype(jnp.bfloat16)).astype(jnp.float32)

def rms_forward(values, gain_w):
    factor = lax.rsqrt(lax.optimization_barrier(jnp.mean(values * values, axis=-1, keepdims=True)) + epsilon)
    return (values * factor * (1.0 + gain_w), factor)

def rms_backward(values, factor, gain_w, grad_out):
    weighted = grad_out * (1.0 + gain_w)
    inner = lax.optimization_barrier(jnp.mean(weighted * values, axis=-1, keepdims=True))
    grad_in = factor * (weighted - values * factor * factor * inner)
    grad_gain = lax.optimization_barrier(jnp.sum((grad_out * values * factor).reshape(-1, values.shape[-1]), axis=0))
    return (grad_in, grad_gain)

def rotary_tables(positions, width):
    half_width = width // 2
    frequency = theta_base ** (-jnp.arange(half_width, dtype=jnp.float32) * 2.0 / width)
    angles = positions.astype(jnp.float32)[:, None] * frequency[None, :]
    return (jnp.cos(angles)[:, None, :], jnp.sin(angles)[:, None, :])

def rotate(values, cos_tab, sin_tab):
    half_width = values.shape[-1] // 2
    first_half = values[..., :half_width]
    second_half = values[..., half_width:]
    return jnp.concatenate([first_half * cos_tab - second_half * sin_tab, second_half * cos_tab + first_half * sin_tab], axis=-1)

def rotate_back(grads, cos_tab, sin_tab):
    half_width = grads.shape[-1] // 2
    first_half = grads[..., :half_width]
    second_half = grads[..., half_width:]
    return jnp.concatenate([first_half * cos_tab + second_half * sin_tab, second_half * cos_tab - first_half * sin_tab], axis=-1)

def block_positions(block_ids, half_rows):
    offsets = jnp.arange(half_rows, dtype=jnp.int32)
    return (block_ids[:, None] * half_rows + offsets[None, :]).reshape(-1)

def masked_scores(query_block, key_f, pos_block, positions):
    scores = jnp.einsum('qhd,kd->hqk', query_block.astype(jnp.float32), key_f) * HDIM ** (-0.5)
    return jnp.where(positions[None, None, :] <= pos_block[None, :, None], scores, -1e+30)

def attention_forward(query_rot, key_rot, value_bf, positions, block_rows):
    count_blocks = query_rot.shape[0] // block_rows
    key_f = key_rot.astype(jnp.float32)
    value_f = value_bf.astype(jnp.float32)

    def step(carry, item):
        query_block, pos_block = item
        scores = masked_scores(query_block, key_f, pos_block, positions)
        top_score = lax.optimization_barrier(jnp.max(scores, axis=-1, keepdims=True))
        shifted = jnp.exp(scores - top_score)
        totals = lax.optimization_barrier(jnp.sum(shifted, axis=-1, keepdims=True))
        probs = shifted / totals
        log_total = top_score[..., 0] + jnp.log(totals[..., 0])
        attn_block = jnp.einsum('hqk,kd->qhd', rounded(probs), value_f)
        return (carry, (attn_block.astype(jnp.bfloat16), log_total))
    items = (query_rot.reshape(count_blocks, block_rows, HEADS, HDIM), positions.reshape(count_blocks, block_rows))
    _, (attn_blocks, log_blocks) = lax.scan(step, jnp.zeros((), jnp.float32), items)
    return (attn_blocks.reshape(-1, HEADS * HDIM), log_blocks)

def attention_backward(query_rot, key_rot, value_bf, positions, grad_attn, attn_out, log_blocks, block_rows):
    count_blocks = query_rot.shape[0] // block_rows
    key_f = key_rot.astype(jnp.float32)
    value_f = value_bf.astype(jnp.float32)
    grad_heads = grad_attn.reshape(-1, HEADS, HDIM)
    delta = lax.optimization_barrier(jnp.sum(grad_heads.astype(jnp.float32) * attn_out.reshape(-1, HEADS, HDIM).astype(jnp.float32), axis=-1))
    delta_blocks = delta.reshape(count_blocks, block_rows, HEADS).transpose(0, 2, 1)

    def step(carry, item):
        grad_key, grad_value = carry
        query_block, pos_block, grad_block, log_block, delta_block = item
        scores = masked_scores(query_block, key_f, pos_block, positions)
        probs_again = jnp.exp(scores - log_block[:, :, None])
        grad_f = grad_block.astype(jnp.float32)
        grad_probs = jnp.einsum('qhd,kd->hqk', grad_f, value_f)
        grad_scores = rounded(probs_again * (grad_probs - delta_block[:, :, None]))
        grad_query = jnp.einsum('hqk,kd->qhd', grad_scores, key_f) * HDIM ** (-0.5)
        grad_key = grad_key + jnp.einsum('hqk,qhd->kd', grad_scores, query_block.astype(jnp.float32)) * HDIM ** (-0.5)
        grad_value = grad_value + jnp.einsum('hqk,qhd->kd', rounded(probs_again), grad_f)
        return ((grad_key, grad_value), grad_query)
    zeros_kv = jnp.zeros((query_rot.shape[0], HDIM), jnp.float32)
    items = (query_rot.reshape(count_blocks, block_rows, HEADS, HDIM), positions.reshape(count_blocks, block_rows), grad_heads.reshape(count_blocks, block_rows, HEADS, HDIM), log_blocks, delta_blocks)
    (grad_key, grad_value), grad_query = lax.scan(step, (zeros_kv, zeros_kv), items)
    return (grad_query.reshape(-1, HEADS, HDIM), grad_key, grad_value)

def dot_f32(left, right):
    return jnp.dot(left, right, preferred_element_type=jnp.float32)

def reference(block_input, cotangent, pair_blocks, w_query, w_key, w_value, w_out, w_gate, w_up, w_down, attn_pre_gain, query_gain, key_gain, attn_post_gain, ffw_pre_gain, ffw_post_gain):
    half_rows = TOK_DEV // 2
    positions = block_positions(pair_blocks.reshape(-1), half_rows)
    cos_tab, sin_tab = rotary_tables(positions, HDIM)
    block_rows = min(512, SEQ)
    gain_one = attn_pre_gain.astype(jnp.float32)
    gain_query = query_gain.astype(jnp.float32)
    gain_key = key_gain.astype(jnp.float32)
    gain_two = attn_post_gain.astype(jnp.float32)
    gain_three = ffw_pre_gain.astype(jnp.float32)
    gain_four = ffw_post_gain.astype(jnp.float32)
    grad_sums = None
    outputs = []
    input_grads = []
    for seq_index in range(N_WSH):
        resid_in = block_input[seq_index].astype(jnp.float32)
        grad_top = cotangent[seq_index]
        normed_one, factor_one = rms_forward(resid_in, gain_one)
        attn_in = normed_one.astype(jnp.bfloat16)
        query_raw = dot_f32(attn_in, w_query).reshape(SEQ, HEADS, HDIM)
        key_raw = dot_f32(attn_in, w_key)[:, None, :]
        value_bf = dot_f32(attn_in, w_value).astype(jnp.bfloat16)
        query_normed, query_factor = rms_forward(query_raw, gain_query)
        key_normed, key_factor = rms_forward(key_raw, gain_key)
        query_rot = rotate(query_normed, cos_tab, sin_tab).astype(jnp.bfloat16)
        key_rot = rotate(key_normed, cos_tab, sin_tab)[:, 0, :].astype(jnp.bfloat16)
        attn_out, log_blocks = attention_forward(query_rot, key_rot, value_bf, positions, block_rows)
        attn_proj = dot_f32(attn_out, w_out)
        normed_two, factor_two = rms_forward(attn_proj, gain_two)
        mid = resid_in + normed_two
        normed_three, factor_three = rms_forward(mid, gain_three)
        ffw_in = normed_three.astype(jnp.bfloat16)
        gate = dot_f32(ffw_in, w_gate)
        up_val = dot_f32(ffw_in, w_up)
        activated, gelu_back = jax.vjp(lambda inner: jax.nn.gelu(inner, approximate=True), gate)
        hidden = (activated * up_val).astype(jnp.bfloat16)
        ffw_proj = dot_f32(hidden, w_down)
        normed_four, factor_four = rms_forward(ffw_proj, gain_four)
        outputs.append(mid + normed_four)
        grad_ffw, grad_gain_four = rms_backward(ffw_proj, factor_four, gain_four, grad_top)
        grad_ffw_bf = grad_ffw.astype(jnp.bfloat16)
        grad_w_down = dot_f32(hidden.T, grad_ffw_bf)
        grad_hidden = dot_f32(grad_ffw_bf, w_down.T)
        grad_gate = gelu_back(grad_hidden * up_val)[0].astype(jnp.bfloat16)
        grad_up = (grad_hidden * activated).astype(jnp.bfloat16)
        grad_w_gate = dot_f32(ffw_in.T, grad_gate)
        grad_w_up = dot_f32(ffw_in.T, grad_up)
        grad_ffw_in = dot_f32(grad_gate, w_gate.T) + dot_f32(grad_up, w_up.T)
        grad_mid_part, grad_gain_three = rms_backward(mid, factor_three, gain_three, grad_ffw_in)
        grad_mid = grad_top + grad_mid_part
        grad_proj, grad_gain_two = rms_backward(attn_proj, factor_two, gain_two, grad_mid)
        grad_proj_bf = grad_proj.astype(jnp.bfloat16)
        grad_w_out = dot_f32(attn_out.T, grad_proj_bf)
        grad_attn = dot_f32(grad_proj_bf, w_out.T).astype(jnp.bfloat16)
        grad_query, grad_key, grad_value = attention_backward(query_rot, key_rot, value_bf, positions, grad_attn, attn_out, log_blocks, block_rows)
        grad_query_raw, grad_gain_query = rms_backward(query_raw, query_factor, gain_query, rotate_back(grad_query, cos_tab, sin_tab))
        grad_key_raw, grad_gain_key = rms_backward(key_raw, key_factor, gain_key, rotate_back(grad_key[:, None, :], cos_tab, sin_tab))
        grad_query_bf = grad_query_raw.reshape(SEQ, HEADS * HDIM).astype(jnp.bfloat16)
        grad_key_bf = grad_key_raw[:, 0, :].astype(jnp.bfloat16)
        grad_value_bf = grad_value.astype(jnp.bfloat16)
        grad_w_query = dot_f32(attn_in.T, grad_query_bf)
        grad_w_key = dot_f32(attn_in.T, grad_key_bf)
        grad_w_value = dot_f32(attn_in.T, grad_value_bf)
        grad_attn_in = dot_f32(grad_query_bf, w_query.T) + dot_f32(grad_key_bf, w_key.T) + dot_f32(grad_value_bf, w_value.T)
        grad_in_part, grad_gain_one = rms_backward(resid_in, factor_one, gain_one, grad_attn_in)
        input_grads.append(grad_mid + grad_in_part)
        current = (grad_w_query, grad_w_key, grad_w_value, grad_w_out, grad_w_gate, grad_w_up, grad_w_down, grad_gain_one, grad_gain_query, grad_gain_key, grad_gain_two, grad_gain_three, grad_gain_four)
        if grad_sums is None:
            grad_sums = current
        else:
            grad_sums = tuple((total + extra for total, extra in zip(grad_sums, current)))
    return (jnp.stack(outputs), jnp.stack(input_grads), grad_sums[0], grad_sums[1], grad_sums[2], grad_sums[3], grad_sums[4], grad_sums[5], grad_sums[6], grad_sums[7], grad_sums[8], grad_sums[9], grad_sums[10], grad_sums[11], grad_sums[12])
```

```python
import jax
import jax.numpy as jnp
from jax import lax
from jax.experimental import pallas as pl
from jax.experimental.pallas import tpu as pltpu
from jax.sharding import PartitionSpec as P

HEADS = 4
HDIM = 256
SCALE = HDIM ** (-0.5)
RANKS = 64
BITS = 6
HALF = 64
KV_PARTS = (48, 48, 48, 48, 32, 32)
KV_OFFS = (0, 48, 96, 144, 192, 224)
F32 = jnp.float32
BF16 = jnp.bfloat16


epsilon = 1e-06
theta_base = 1000000.0


def gray(rank):
    return rank ^ ((rank >> 1) & 21)


BIT_PERMS = [
    [(r, gray(gray(r) ^ (1 << bit))) for r in range(RANKS)] for bit in range(BITS)
]


def swap_bit(values, bit):
    return lax.ppermute(values, "ctx", BIT_PERMS[bit])


def swap_core(values):
    return lax.ppermute(values, "wsh", [(0, 1), (1, 0)])


def rms_forward(values, gain_w):
    factor = lax.rsqrt(jnp.mean(values * values, axis=-1, keepdims=True) + epsilon)
    return (values * factor * (1.0 + gain_w), factor)


def rms_backward(values, factor, gain_w, grad_out):
    weighted = grad_out * (1.0 + gain_w)
    inner = jnp.mean(weighted * values, axis=-1, keepdims=True)
    grad_in = factor * (weighted - values * factor * factor * inner)
    grad_gain = jnp.sum((grad_out * values * factor).reshape(-1, values.shape[-1]), axis=0)
    return (grad_in, grad_gain)


def rotary_tables(positions, width):
    half_width = width // 2
    frequency = theta_base ** (-jnp.arange(half_width, dtype=F32) * 2.0 / width)
    angles = positions.astype(F32)[:, None] * frequency[None, :]
    return (jnp.cos(angles)[:, None, :], jnp.sin(angles)[:, None, :])


def rotate(values, cos_tab, sin_tab):
    half_width = values.shape[-1] // 2
    a = values[..., :half_width]
    b = values[..., half_width:]
    return jnp.concatenate([a * cos_tab - b * sin_tab, b * cos_tab + a * sin_tab], axis=-1)


def rotate_back(grads, cos_tab, sin_tab):
    half_width = grads.shape[-1] // 2
    a = grads[..., :half_width]
    b = grads[..., half_width:]
    return jnp.concatenate([a * cos_tab + b * sin_tab, b * cos_tab - a * sin_tab], axis=-1)


def block_positions(block_ids, half_rows):
    offsets = jnp.arange(half_rows, dtype=jnp.int32)
    return (block_ids[:, None] * half_rows + offsets[None, :]).reshape(-1)


def dot_f32(left, right):
    return jnp.dot(left, right, preferred_element_type=F32)


def dot_nt(left, right):
    return lax.dot_general(left, right, (((1,), (1,)), ((), ())), preferred_element_type=F32)


def dot_tn(left, right):
    return lax.dot_general(left, right, (((0,), (0,)), ((), ())), preferred_element_type=F32)


def fill_table(pairs, code, table):
    def body(dist, carry):
        owner = gray(code ^ dist)
        for half in range(2):
            block = pairs[owner * 2 + half]
            for part in range(BITS):
                slot = ((dist >> part) | (dist << (BITS - part))) & (RANKS - 1)
                table[part, block] = slot * 2 + half
        return carry

    lax.fori_loop(0, RANKS, body, 0)


def load_chunk(kv_refs, table, chunk):
    keys, values = [], []
    for sub in range(4):
        rows = jnp.concatenate(
            [kv_refs[part][table[part, chunk * 4 + sub]] for part in range(BITS)], axis=0
        )
        keys.append(jnp.concatenate([rows[0:64], rows[64:128]], axis=1))
        values.append(jnp.concatenate([rows[128:192], rows[192:256]], axis=1))
    return jnp.concatenate(keys, axis=0), jnp.concatenate(values, axis=0)


def low_high(pairs, mine):
    first = pairs[mine * 2]
    second = pairs[mine * 2 + 1]
    low = jnp.where(first < second, 0, 1)
    low_block = jnp.minimum(first, second)
    high_block = jnp.maximum(first, second)
    return low, low_block, high_block


def attn_fwd_kernel(pairs, ids, q_ref, *refs):
    kv_refs = refs[:BITS]
    out_ref, lse_ref, acc_ref, sum_ref, table = refs[BITS:]
    mine = ids[0]
    fill_table(pairs, gray(mine), table)
    low, low_block, high_block = low_high(pairs, mine)
    acc_ref[...] = jnp.zeros_like(acc_ref)
    sum_ref[...] = jnp.zeros_like(sum_ref)
    tok = lax.broadcasted_iota(jnp.int32, (256, 256), 0) & (HALF - 1)
    lane = lax.broadcasted_iota(jnp.int32, (256, 256), 1)
    gap = lane - tok

    def tile(half, block, chunk, keys, values):
        scores = dot_nt(q_ref[half], keys)
        probs = jnp.where(gap <= block * HALF - chunk * 256, jnp.exp(scores), 0.0)
        sum_ref[half] += probs[:, :128] + probs[:, 128:]
        acc_ref[half] += dot_f32(probs.astype(BF16), values)

    def both(chunk, carry):
        keys, values = load_chunk(kv_refs, table, chunk)
        tile(low, low_block, chunk, keys, values)
        tile(1 - low, high_block, chunk, keys, values)
        return carry

    def upper(chunk, carry):
        keys, values = load_chunk(kv_refs, table, chunk)
        tile(1 - low, high_block, chunk, keys, values)
        return carry

    n_low = low_block // 4 + 1
    n_high = high_block // 4 + 1
    lax.fori_loop(0, n_low, both, 0)
    lax.fori_loop(n_low, n_high, upper, 0)
    for half in range(2):
        total = jnp.sum(sum_ref[half], axis=-1, keepdims=True)
        out_ref[half] = (acc_ref[half] / total).astype(BF16)
        lse_ref[half] = jnp.broadcast_to(jnp.log(total), (256, 128))


def attn_bwd_kernel(pairs, ids, q_ref, go_ref, lse_ref, delta_ref, *refs):
    kv_refs = refs[:BITS]
    gq_ref = refs[BITS]
    gkv_refs = refs[BITS + 1 : 2 * BITS + 1]
    table = refs[2 * BITS + 1]
    mine = ids[0]
    fill_table(pairs, gray(mine), table)
    low, low_block, high_block = low_high(pairs, mine)
    gq_ref[...] = jnp.zeros_like(gq_ref)
    tok = lax.broadcasted_iota(jnp.int32, (256, 256), 1) & (HALF - 1)
    row = lax.broadcasted_iota(jnp.int32, (256, 256), 0)
    gap = row - tok

    def tile(half, block, chunk, keys, values):
        scores = dot_nt(keys, q_ref[half])
        probs = jnp.exp(scores - lse_ref[half][0:1])
        probs = jnp.where(gap <= block * HALF - chunk * 256, probs, 0.0)
        grad_probs = dot_nt(values, go_ref[half])
        grad_scores = (probs * (grad_probs - delta_ref[half][0:1])).astype(BF16)
        grad_value = dot_f32(probs.astype(BF16), go_ref[half])
        grad_key = dot_f32(grad_scores, q_ref[half])
        gq_ref[half] += dot_tn(grad_scores, keys)
        return grad_key, grad_value

    def store(chunk, grad_key, grad_value):
        grad_key = grad_key.astype(BF16)
        grad_value = grad_value.astype(BF16)
        for sub in range(4):
            gk = grad_key[sub * 64 : sub * 64 + 64]
            gv = grad_value[sub * 64 : sub * 64 + 64]
            rows = jnp.concatenate([gk[:, :128], gk[:, 128:], gv[:, :128], gv[:, 128:]], axis=0)
            for part in range(BITS):
                off = KV_OFFS[part]
                gkv_refs[part][table[part, chunk * 4 + sub]] = rows[off : off + KV_PARTS[part]]

    def both(chunk, carry):
        keys, values = load_chunk(kv_refs, table, chunk)
        gk0, gv0 = tile(low, low_block, chunk, keys, values)
        gk1, gv1 = tile(1 - low, high_block, chunk, keys, values)
        store(chunk, gk0 + gk1, gv0 + gv1)
        return carry

    def upper(chunk, carry):
        keys, values = load_chunk(kv_refs, table, chunk)
        gk1, gv1 = tile(1 - low, high_block, chunk, keys, values)
        store(chunk, gk1, gv1)
        return carry

    def empty(chunk, carry):
        zeros = jnp.zeros((256, 256), F32)
        store(chunk, zeros, zeros)
        return carry

    n_low = low_block // 4 + 1
    n_high = high_block // 4 + 1
    lax.fori_loop(0, n_low, both, 0)
    lax.fori_loop(n_low, n_high, upper, 0)
    lax.fori_loop(n_high, 32, empty, 0)


VM = pl.BlockSpec(memory_space=pltpu.VMEM)
SM = pl.BlockSpec(memory_space=pltpu.SMEM)


def attention_forward(pairs, ids, query, kv_parts):
    return pl.pallas_call(
        attn_fwd_kernel,
        out_shape=(
            jax.ShapeDtypeStruct((2, 256, 256), BF16),
            jax.ShapeDtypeStruct((2, 256, 128), F32),
        ),
        in_specs=[SM, SM, VM] + [VM] * BITS,
        out_specs=(VM, VM),
        scratch_shapes=[
            pltpu.VMEM((2, 256, 256), F32),
            pltpu.VMEM((2, 256, 128), F32),
            pltpu.SMEM((BITS, 128), jnp.int32),
        ],
        name="attn_fwd",
    )(pairs, ids, query, *kv_parts)


def attention_backward(pairs, ids, query, grad_out, lse, delta, kv_parts):
    outs = pl.pallas_call(
        attn_bwd_kernel,
        out_shape=(jax.ShapeDtypeStruct((2, 256, 256), F32),)
        + tuple(jax.ShapeDtypeStruct((128, rows, 128), BF16) for rows in KV_PARTS),
        in_specs=[SM, SM, VM, VM, VM, VM] + [VM] * BITS,
        out_specs=(VM,) * (BITS + 1),
        scratch_shapes=[pltpu.SMEM((BITS, 128), jnp.int32)],
        name="attn_bwd",
    )(pairs, ids, query, grad_out, lse, delta, *kv_parts)
    return outs[0], outs[1:]


def head_rows(values):
    return (
        values.reshape(2, HALF, HEADS, HDIM).transpose(0, 2, 1, 3).reshape(2, HEADS * HALF, HDIM)
    )


def token_rows(values):
    return values.reshape(2, HEADS, HALF, HDIM).transpose(0, 2, 1, 3).reshape(128, HEADS, HDIM)


def gather_kv(key_rot, value_bf):
    both = jnp.concatenate([key_rot, value_bf], axis=1)
    rows = both.reshape(2, HALF, 4, 128).transpose(0, 2, 1, 3).reshape(2, 256, 128)
    parts = [rows[:, off : off + size] for off, size in zip(KV_OFFS, KV_PARTS)]
    for step in range(BITS):
        parts = [
            jnp.concatenate([part, swap_bit(part, (index + step) % BITS)], axis=0)
            for index, part in enumerate(parts)
        ]
    return parts


def scatter_kv(parts):
    parts = list(parts)
    for step in reversed(range(BITS)):
        for index in range(BITS):
            part = parts[index]
            size = part.shape[0] // 2
            moved = swap_bit(part[size:].astype(BF16), (index + step) % BITS)
            parts[index] = part[:size].astype(F32) + moved.astype(F32)
    rows = jnp.concatenate(parts, axis=1)
    return rows.reshape(2, 4, HALF, 128).transpose(0, 2, 1, 3).reshape(128, 512)


def sum_chunks(parts, code):
    parts = list(parts)
    for step in reversed(range(BITS)):
        for index in range(BITS):
            part = parts[index]
            bit = (index + step) % BITS
            mine = (code >> bit) & 1
            size = part.shape[0] // 2
            sent = lax.dynamic_slice_in_dim(part, (1 - mine) * size, size, 0)
            kept = lax.dynamic_slice_in_dim(part, mine * size, size, 0)
            moved = swap_bit(sent.astype(BF16), bit)
            parts[index] = kept.astype(F32) + moved.astype(F32)
    parts = [part.astype(BF16) for part in parts]
    for step in range(BITS):
        for index in range(BITS):
            part = parts[index]
            bit = (index + step) % BITS
            mine = ((code >> bit) & 1) == 1
            moved = swap_bit(part, bit)
            parts[index] = jnp.concatenate(
                [jnp.where(mine, moved, part), jnp.where(mine, part, moved)], axis=0
            )
    return parts


def split_rows(rows, sizes):
    parts, off = [], 0
    for size in sizes:
        parts.append(rows[:, off : off + size])
        off += size
    return parts


def to_chunks(grad, row_groups):
    rows, cols = grad.shape
    blocks = cols // 128
    per = rows // row_groups
    if row_groups * blocks == RANKS:
        return grad.reshape(row_groups, per, blocks, 128).transpose(0, 2, 1, 3).reshape(RANKS, per, 128)
    return grad.reshape(RANKS, per, blocks, 128).transpose(0, 2, 1, 3).reshape(RANKS, per * blocks, 128)


def from_chunks(chunks, rows, cols, row_groups):
    blocks = cols // 128
    per = rows // row_groups
    if row_groups * blocks == RANKS:
        return chunks.reshape(row_groups, blocks, per, 128).transpose(0, 2, 1, 3).reshape(rows, cols)
    return chunks.reshape(RANKS, blocks, per, 128).transpose(0, 2, 1, 3).reshape(rows, cols)


def per_device(
    block_input,
    cotangent,
    pair_blocks,
    w_query,
    w_key,
    w_value,
    w_out,
    w_gate,
    w_up,
    w_down,
    attn_pre_gain,
    query_gain,
    key_gain,
    attn_post_gain,
    ffw_pre_gain,
    ffw_post_gain,
):
    row_count = block_input.shape[1]
    my_rank = lax.axis_index("ctx")
    core = lax.axis_index("wsh")
    first_core = core == 0
    code = gray(my_rank)
    ids = my_rank.reshape(1).astype(jnp.int32)
    pairs = pair_blocks.reshape(-1)

    def in_order(mine, other, axis=-1):
        return jnp.concatenate(
            [jnp.where(first_core, mine, other), jnp.where(first_core, other, mine)], axis=axis
        )

    gains = (attn_pre_gain, query_gain, key_gain, attn_post_gain, ffw_pre_gain, ffw_post_gain)
    gain_sizes = [320, 128, 128, 320, 320, 320]
    gains_mine = jnp.concatenate(gains)
    gains_other = swap_core(gains_mine)
    key_value_w = jnp.concatenate([w_key, w_value], axis=1)
    key_value_o = swap_core(key_value_w)
    query_o = swap_core(w_query)
    out_o = swap_core(w_out)
    gate_o = swap_core(w_gate)
    up_o = swap_core(w_up)
    down_o = swap_core(w_down)
    full_gains, off = [], 0
    for size in gain_sizes:
        full_gains.append(
            in_order(gains_mine[off : off + size], gains_other[off : off + size]).astype(F32)
        )
        off += size
    gain_one, gain_query, gain_key, gain_two, gain_three, gain_four = full_gains

    resid_in = block_input[0].astype(F32)
    grad_top = cotangent[0]
    my_blocks = lax.dynamic_slice_in_dim(pair_blocks, my_rank, 1, 0)[0]
    query_pos = block_positions(my_blocks, HALF)
    cos_tab, sin_tab = rotary_tables(query_pos, HDIM)

    normed_one, factor_one = rms_forward(resid_in, gain_one)
    attn_in = normed_one.astype(BF16)
    kv_mine = dot_f32(attn_in, key_value_w)
    kv_other = dot_f32(attn_in, key_value_o)
    key_raw = in_order(kv_mine[:, :128], kv_other[:, :128])[:, None, :]
    value_bf = in_order(kv_mine[:, 128:], kv_other[:, 128:]).astype(BF16)
    key_normed, key_factor = rms_forward(key_raw, gain_key)
    key_rot = rotate(key_normed, cos_tab, sin_tab)[:, 0, :].astype(BF16)
    kv_parts = gather_kv(key_rot, value_bf)

    query_raw = jnp.concatenate(
        [dot_f32(attn_in, w_query), dot_f32(attn_in, query_o)], axis=1
    ).reshape(row_count, HEADS, HDIM)
    query_normed, query_factor = rms_forward(query_raw, gain_query)
    query_rot = (rotate(query_normed, cos_tab, sin_tab).astype(BF16) * SCALE).astype(BF16)
    query_rows = head_rows(query_rot.reshape(row_count, HEADS * HDIM))

    out_rows, lse = attention_forward(pairs, ids, query_rows, kv_parts)
    lse_row = jnp.broadcast_to(lse[:, :, 0][:, None, :], (2, 8, 256))
    attn_heads = token_rows(out_rows)
    attn_out = attn_heads.reshape(row_count, HEADS * HDIM)
    attn_proj = dot_f32(attn_out[:, :512], w_out) + dot_f32(attn_out[:, 512:], out_o)
    normed_two, factor_two = rms_forward(attn_proj, gain_two)
    mid = resid_in + normed_two
    normed_three, factor_three = rms_forward(mid, gain_three)
    ffw_in = normed_three.astype(BF16)
    gate = jnp.concatenate([dot_f32(ffw_in, w_gate), dot_f32(ffw_in, gate_o)], axis=1)
    up_val = jnp.concatenate([dot_f32(ffw_in, w_up), dot_f32(ffw_in, up_o)], axis=1)
    activated, gelu_back = jax.vjp(lambda inner: jax.nn.gelu(inner, approximate=True), gate)
    hidden = (activated * up_val).astype(BF16)
    ffw_proj = dot_f32(hidden[:, :1024], w_down) + dot_f32(hidden[:, 1024:], down_o)
    normed_four, factor_four = rms_forward(ffw_proj, gain_four)
    block_output = mid + normed_four

    grad_ffw, grad_gain_four = rms_backward(ffw_proj, factor_four, gain_four, grad_top)
    grad_ffw_bf = grad_ffw.astype(BF16)
    grad_hidden = jnp.concatenate([dot_nt(grad_ffw_bf, w_down), dot_nt(grad_ffw_bf, down_o)], axis=1)
    grad_gate = gelu_back(grad_hidden * up_val)[0].astype(BF16)
    grad_up = (grad_hidden * activated).astype(BF16)
    grad_ffw_in = (
        dot_nt(grad_gate[:, :1024], w_gate)
        + dot_nt(grad_gate[:, 1024:], gate_o)
        + dot_nt(grad_up[:, :1024], w_up)
        + dot_nt(grad_up[:, 1024:], up_o)
    )
    grad_mid_part, grad_gain_three = rms_backward(mid, factor_three, gain_three, grad_ffw_in)
    grad_mid = grad_top + grad_mid_part
    grad_proj, grad_gain_two = rms_backward(attn_proj, factor_two, gain_two, grad_mid)
    grad_proj_bf = grad_proj.astype(BF16)
    grad_attn = jnp.concatenate([dot_nt(grad_proj_bf, w_out), dot_nt(grad_proj_bf, out_o)], axis=1).astype(
        BF16
    )
    grad_rows = head_rows(grad_attn)
    delta = jnp.sum(grad_rows.astype(F32) * out_rows.astype(F32), axis=-1)
    delta_row = jnp.broadcast_to(delta[:, None, :], (2, 8, 256))

    early = jnp.concatenate(
        [
            ffw_in,
            grad_ffw_bf,
            grad_proj_bf,
            grad_gate[:, 1024:],
            grad_up[:, 1024:],
            hidden[:, 1024:],
            attn_out[:, 512:],
        ],
        axis=1,
    )
    early_o = swap_core(early)

    def pair_tokens(mine, start, size):
        return jnp.concatenate([mine, early_o[:, start : start + size]], axis=0)

    ffw_in_2 = pair_tokens(ffw_in, 0, 640)
    grad_ffw_2 = pair_tokens(grad_ffw_bf, 640, 640)
    grad_proj_2 = pair_tokens(grad_proj_bf, 1280, 640)
    grad_w_gate = dot_tn(ffw_in_2, pair_tokens(grad_gate[:, :1024], 1920, 1024))
    grad_w_up = dot_tn(ffw_in_2, pair_tokens(grad_up[:, :1024], 2944, 1024))
    grad_w_down = dot_tn(pair_tokens(hidden[:, :1024], 3968, 1024), grad_ffw_2)
    grad_w_out = dot_tn(pair_tokens(attn_out[:, :512], 4992, 512), grad_proj_2)
    early_rows = jnp.concatenate(
        [
            to_chunks(grad_w_gate, 8),
            to_chunks(grad_w_up, 8),
            to_chunks(grad_w_down, 64),
            to_chunks(grad_w_out, 64),
        ],
        axis=1,
    ).astype(BF16)
    early_sums = jnp.concatenate(
        sum_chunks(split_rows(early_rows, (48, 48, 48, 48, 48, 40)), code), axis=1
    )
    sum_gate = from_chunks(early_sums[:, 0:80], 640, 1024, 8).astype(F32)
    sum_up = from_chunks(early_sums[:, 80:160], 640, 1024, 8).astype(F32)
    sum_down = from_chunks(early_sums[:, 160:240], 1024, 640, 64).astype(F32)
    sum_out = from_chunks(early_sums[:, 240:280], 512, 640, 64).astype(F32)

    grad_query_rows, grad_kv_parts = attention_backward(
        pairs, ids, query_rows, grad_rows, lse_row, delta_row, kv_parts
    )
    grad_query = token_rows(grad_query_rows) * SCALE
    kv_grad = scatter_kv(grad_kv_parts)
    grad_key = kv_grad[:, :HDIM]
    grad_value = kv_grad[:, HDIM:]
    grad_query_raw, grad_gain_query = rms_backward(
        query_raw, query_factor, gain_query, rotate_back(grad_query, cos_tab, sin_tab)
    )
    grad_key_raw, grad_gain_key = rms_backward(
        key_raw, key_factor, gain_key, rotate_back(grad_key[:, None, :], cos_tab, sin_tab)
    )
    grad_query_bf = grad_query_raw.reshape(row_count, HEADS * HDIM).astype(BF16)
    grad_key_bf = grad_key_raw[:, 0, :].astype(BF16)
    grad_value_bf = grad_value.astype(BF16)

    def my_half(values):
        return jnp.where(first_core, values[..., :128], values[..., 128:])

    def other_half(values):
        return jnp.where(first_core, values[..., 128:], values[..., :128])

    kv_grad_mine = jnp.concatenate([my_half(grad_key_bf), my_half(grad_value_bf)], axis=1)
    kv_grad_other = jnp.concatenate([other_half(grad_key_bf), other_half(grad_value_bf)], axis=1)
    grad_attn_in = (
        dot_nt(grad_query_bf[:, :512], w_query)
        + dot_nt(grad_query_bf[:, 512:], query_o)
        + dot_nt(kv_grad_mine, key_value_w)
        + dot_nt(kv_grad_other, key_value_o)
    )
    grad_in_part, grad_gain_one = rms_backward(resid_in, factor_one, gain_one, grad_attn_in)
    input_grad = grad_mid + grad_in_part

    late_o = swap_core(jnp.concatenate([attn_in, grad_query_bf[:, 512:], kv_grad_other], axis=1))
    attn_in_2 = jnp.concatenate([attn_in, late_o[:, :640]], axis=0)
    grad_query_2 = jnp.concatenate([grad_query_bf[:, :512], late_o[:, 640:1152]], axis=0)
    kv_grad_2 = jnp.concatenate([kv_grad_mine, late_o[:, 1152:]], axis=0)
    grad_w_query = dot_tn(attn_in_2, grad_query_2)
    grad_w_kv = dot_tn(attn_in_2, kv_grad_2)

    gain_grads = (
        grad_gain_one,
        grad_gain_query,
        grad_gain_key,
        grad_gain_two,
        grad_gain_three,
        grad_gain_four,
    )

    def half_of(values, low):
        size = values.shape[0] // 2
        return jnp.where(low, values[:size], values[size:])

    gains_keep = jnp.concatenate([half_of(g, first_core) for g in gain_grads])
    gains_send = jnp.concatenate([half_of(g, jnp.logical_not(first_core)) for g in gain_grads])
    gains_sum = (gains_keep + swap_core(gains_send)).reshape(12, 128)
    kv_rows = grad_w_kv.reshape(640, 2, 128).transpose(1, 0, 2).reshape(1280, 128)
    kv_rows = jnp.concatenate([kv_rows, gains_sum, jnp.zeros((244, 128), F32)], axis=0)
    late_rows = jnp.concatenate(
        [to_chunks(grad_w_query, 16), kv_rows.reshape(RANKS, 24, 128)], axis=1
    ).astype(BF16)
    late_sums = jnp.concatenate(
        sum_chunks(split_rows(late_rows, (16, 16, 8, 8, 8, 8)), code), axis=1
    )
    sum_query = from_chunks(late_sums[:, :40], 640, 512, 16).astype(F32)
    kv_sums = late_sums[:, 40:].reshape(1536, 128).astype(F32)
    sum_key = kv_sums[:640]
    sum_value = kv_sums[640:1280]
    gain_sums = kv_sums[1280:1292].reshape(1536)
    gain_outs, off = [], 0
    for size in gain_sizes:
        gain_outs.append(gain_sums[off : off + size])
        off += size
    return (
        block_output[None],
        input_grad[None],
        sum_query,
        sum_key,
        sum_value,
        sum_out,
        sum_gate,
        sum_up,
        sum_down,
    ) + tuple(gain_outs)


def solution(mesh):
    weights = (
        P(None, "wsh"),
        P(None, "wsh"),
        P(None, "wsh"),
        P("wsh", None),
        P(None, "wsh"),
        P(None, "wsh"),
        P("wsh", None),
    ) + (P("wsh"),) * 6
    return jax.shard_map(
        per_device,
        mesh=mesh,
        in_specs=(P("wsh", "ctx", None), P("wsh", "ctx", None), P()) + weights,
        out_specs=(P("wsh", "ctx", None), P("wsh", "ctx", None)) + weights,
        check_vma=False,
    )
```
